32 devices in a mesh: clip: 2 (over core), tm: 8 (over z, x), head: 2 (over y).
Axes of the slice: x: 2, y: 2, z: 4, core: 2. Of those that a mesh axis runs over, the one named last changes fastest.
Arguments:
- video_tokens: bfloat16 [32, 1568, 1024], P(('clip', 'tm')), parts along dimension 0, may hold values from -6 to 6
- window_order: int32 [32, 1568], P(('clip', 'tm')), parts along dimension 0, may hold values from 0 to 1567, each once within a row
- clip_id: int32 [32], P(('clip', 'tm')), parts along dimension 0, may hold values from 0 to 3, never falling along the last dimension, each value on 1 to 8 neighbouring positions
- attend_weight: bfloat16 [3, 1024, 1024], P(None, None, 'head'), may hold values from -0.75 to 0.75
- attend_out: bfloat16 [1024, 1024], P('head'), may hold values from -0.1875 to 0.1875
- recur_weight: bfloat16 [3, 1024, 1024], P(None, None, 'head'), may hold values from -0.1875 to 0.1875
- frame_decay: float32 [32, 1024], P(('clip', 'tm'), 'head'), parts along dimension 0, may hold values from -5.7 to -0.02125, as said below
- recur_out: bfloat16 [1024, 1024], P('head'), may hold values from -0.1875 to 0.1875
Outputs:
- features_out: bfloat16 [32, 1568, 1024], P(('clip', 'tm'), None, 'head'), parts along dimension 0
The draws below stay inside these ranges and needn't reach their ends.
There are 2 independent parts, one for each index of `clip`. The reference program is written for one: setup_inputs(seed, part) draws one part's arguments, and reference() takes and returns one part's arrays. A program takes and returns all parts, laid end to end along the dimension named above; an argument that names none is the same for every part. Nothing has to cross between parts.
Inputs may be any that keep to these rules, and one draw needn't show every extreme that they name: `clip_id`: never falls along the frames; a clip spans 1 to 8 frames. `frame_decay`: negative.
All inputs are finite; a program needn't handle non-finite values.
Results may differ from the reference program's by a relative error of at most 0.01.
Values may be sent and summed in bfloat16 or wider, within the bound.
A program may use at most 128 MiB of HBM per device.

```python
import math
import jax
import jax.numpy as jnp
import numpy as np
from jax import lax

HEAD_DIMENSION = 64
WINDOW = 49
MODEL_DIMENSION = 1024
F_DEV = 2
TOKF = 1568
FRAME_TOTAL = 16
N_TM = 8
N_HEAD = 2


def draw_attend_weight(key, part):
    first_key, second_key, third_key = jax.random.split(jax.random.fold_in(key, 11), 3)
    shared = jnp.clip(jax.random.normal(first_key, (MODEL_DIMENSION, MODEL_DIMENSION), jnp.float32), -4.0, 4.0)
    random_perturbation = jnp.clip(jax.random.normal(second_key, (MODEL_DIMENSION, MODEL_DIMENSION), jnp.float32), -4.0, 4.0)
    value_part = jnp.clip(jax.random.normal(third_key, (MODEL_DIMENSION, MODEL_DIMENSION), jnp.float32), -4.0, 4.0)
    query_part = shared
    key_part = random_perturbation
    return (jnp.stack([query_part, key_part, value_part]) / jnp.sqrt(jnp.float32(MODEL_DIMENSION))).astype(jnp.bfloat16)


def draw_frame_decay(key, part):
    random_child_keys = jax.random.split(jax.random.fold_in(key, 23), 6)
    number_of_heads = MODEL_DIMENSION // HEAD_DIMENSION
    slow_share = 0.5
    slow_head = jax.random.uniform(random_child_keys[0], (number_of_heads,)) < slow_share
    slow_channel = jnp.repeat(slow_head, HEAD_DIMENSION)
    fast_rate = jnp.exp(jax.random.uniform(random_child_keys[1], (MODEL_DIMENSION,), jnp.float32, jnp.log(0.7), jnp.log(2.5)))
    slow_rate = jax.random.uniform(random_child_keys[2], (MODEL_DIMENSION,), jnp.float32, 0.3, 1.0) * 2.3 / FRAME_TOTAL
    default_decay_rate = jnp.where(slow_channel, slow_rate, fast_rate)
    random_perturbation = jnp.exp(jax.random.uniform(random_child_keys[3], (FRAME_TOTAL, MODEL_DIMENSION), jnp.float32, jnp.log(0.5), jnp.log(2.0)))
    spike_head_index = jax.random.uniform(random_child_keys[4], (FRAME_TOTAL, number_of_heads)) < 3.0 / FRAME_TOTAL
    spike_regions = jnp.repeat(spike_head_index, HEAD_DIMENSION, axis=1)
    spike_length = jax.random.uniform(random_child_keys[5], (FRAME_TOTAL, MODEL_DIMENSION), jnp.float32, 0.22, 0.69)
    return -(default_decay_rate[None, :] * random_perturbation + jnp.where(spike_regions, spike_length, 0.0))


def block_scale(key, shape, shards, smallest, top_value):
    def one(position, shards_of):
        draws = jax.random.uniform(jax.random.fold_in(jax.random.fold_in(key, 6), position), (shards_of,), jnp.float32, smallest / len(shards), top_value / len(shards))
        return jnp.repeat(jnp.exp(draws), shape[position] // shards_of).reshape((-1,) + (1,) * (len(shape) - position - 1))

    level = one(*shards[0])
    for cut in shards[1:]:
        level = level * one(*cut)
    return level


def length_profile(number_of, total, limit, lean):
    weights = [(1 << 20) // math.isqrt(grade ** lean) + 1 for grade in range(2, number_of + 1)]
    rest, holding = total - limit - (number_of - 1), [1] * (number_of - 1)
    while rest > 0:
        free = [i for i in range(number_of - 1) if holding[i] < limit]
        pool, left = sum([weights[i] for i in free]), rest
        for i in free:
            addition = min(limit - holding[i], max(1, left * weights[i] // pool), rest)
            holding[i] = holding[i] + addition
            rest = rest - addition
    return np.array([limit] + holding)


def ragged(rng, count, total, limit, lean):
    if count == 2:
        one = jax.random.randint(rng, (), max(1, total - limit), min(limit, total - 1) + 1)
        return jnp.stack([one, total - one])
    sizes = jnp.asarray(length_profile(count, total, limit, lean), jnp.int32)
    couples = (count - 1) // 2
    donor, taker = sizes[1:1 + 2 * couples:2], sizes[2:2 + 2 * couples:2]
    room = jnp.minimum(donor - 1, limit - taker)
    shifted = jax.random.randint(jax.random.fold_in(rng, 1), (couples,), 0, 1 << 20) % (room + 1)
    sizes = sizes.at[1:1 + 2 * couples:2].set(donor - shifted).at[2:2 + 2 * couples:2].set(taker + shifted)
    return sizes[jax.random.permutation(jax.random.fold_in(rng, 2), count)]


def scatter_about(own_key, shape, deviation, bound, cuts=(), kind=jnp.bfloat16):
    entries = deviation * jax.random.normal(own_key, shape, jnp.float32)
    if cuts:
        entries = entries * block_scale(own_key, shape, cuts, -0.22, 0.18)
    return jnp.clip(entries, -bound, bound).astype(kind)


def setup_inputs(seed: int = 0, part: int = 0) -> dict:
    splits = jax.random.split(jax.random.key(seed), 9)
    part_splits = jax.random.split(jax.random.fold_in(splits[8], part), 9)
    return {
        "video_tokens": scatter_about(part_splits[0], (FRAME_TOTAL, TOKF, MODEL_DIMENSION), 1.0, 6.0, ((0, 8),)),
        "window_order": jax.vmap(lambda own: jax.random.permutation(own, TOKF))(jax.random.split(part_splits[1], FRAME_TOTAL)).reshape((FRAME_TOTAL, TOKF)).astype(jnp.int32),
        "clip_id": jnp.searchsorted(jnp.cumsum(ragged(part_splits[2], N_TM // 2, FRAME_TOTAL, 4 * F_DEV, 1)), jnp.arange(FRAME_TOTAL), side="right").astype(jnp.int32),
        "attend_weight": draw_attend_weight(jax.random.fold_in(splits[8], 71), part),
        "attend_out": scatter_about(splits[4], (MODEL_DIMENSION, MODEL_DIMENSION), MODEL_DIMENSION ** -0.5, 0.1875, ((0, 2),)),
        "recur_weight": scatter_about(splits[5], (3, MODEL_DIMENSION, MODEL_DIMENSION), MODEL_DIMENSION ** -0.5, 0.1875, ((2, 2),)),
        "frame_decay": draw_frame_decay(jax.random.fold_in(jax.random.fold_in(splits[8], part), 71), part),
        "recur_out": scatter_about(splits[7], (MODEL_DIMENSION, MODEL_DIMENSION), MODEL_DIMENSION ** -0.5, 0.1875, ((0, 2),)),
    }


EPSILON = 1e-06

def normalize(values):
    return values * lax.rsqrt(lax.optimization_barrier(jnp.mean(values * values, axis=-1, keepdims=True)) + EPSILON)

def window_attention(queries, keys_all, values_all, window_order):
    frame_count, positions, number_of_heads, head_size = queries.shape
    order_index = window_order.astype(jnp.int32)[:, :, None, None]

    def arrange(tensor):
        reordered = jnp.take_along_axis(tensor, order_index, axis=1)
        return reordered.reshape(frame_count, positions // WINDOW, WINDOW, number_of_heads, head_size).astype(jnp.float32)
    scores = jnp.einsum('fwihe,fwjhe->fwhij', arrange(queries), arrange(keys_all)) / jnp.sqrt(jnp.float32(head_size))
    weights = jax.nn.softmax(scores, axis=-1).astype(jnp.bfloat16)
    blended = jnp.einsum('fwhij,fwjhe->fwihe', weights.astype(jnp.float32), arrange(values_all)).astype(jnp.bfloat16)
    blended = blended.reshape(frame_count, positions, number_of_heads, head_size)
    inverse = jnp.argsort(window_order, axis=1).astype(jnp.int32)
    return jnp.take_along_axis(blended, inverse[:, :, None, None], axis=1)

def grouped_product(left_side, right_side):
    group_width = left_side.shape[1] // N_HEAD
    running = jnp.zeros((left_side.shape[0], right_side.shape[1]), jnp.float32)
    for member in range(N_HEAD):
        partial_term = jnp.dot(left_side[:, member * group_width:(member + 1) * group_width], right_side[member * group_width:(member + 1) * group_width], preferred_element_type=jnp.float32)
        rounded = lax.optimization_barrier(partial_term.astype(jnp.bfloat16))
        running = running + rounded.astype(jnp.float32)
    return running

def reference(video_tokens, window_order, clip_id, attend_weight, attend_out, recur_weight, frame_decay, recur_out):
    frame_count, positions, model_width = video_tokens.shape
    number_of_heads = model_width // HEAD_DIMENSION
    inputs = video_tokens.astype(jnp.float32).reshape(-1, model_width)
    normed = normalize(inputs).astype(jnp.bfloat16)
    projected = jnp.einsum('td,kde->kte', normed.astype(jnp.float32), attend_weight.astype(jnp.float32)).astype(jnp.bfloat16)
    shaped = projected.reshape(3, frame_count, positions, number_of_heads, HEAD_DIMENSION)
    attended = window_attention(shaped[0], shaped[1], shaped[2], window_order).reshape(-1, model_width)
    residual = inputs + grouped_product(attended, attend_out)
    normed_again = normalize(residual).astype(jnp.bfloat16)
    recur_proj = jnp.einsum('td,kde->kte', normed_again.astype(jnp.float32), recur_weight.astype(jnp.float32))
    gate_in = jax.nn.sigmoid(recur_proj[0]).reshape(frame_count, positions, model_width)
    value_in = recur_proj[1].reshape(frame_count, positions, model_width)
    out_gate = jax.nn.silu(recur_proj[2]).reshape(frame_count, positions, model_width)
    retain = jnp.exp(frame_decay)
    driven = jnp.sqrt(1.0 - retain * retain)[:, None, :] * gate_in * value_in
    continues = jnp.concatenate([jnp.zeros((1,), jnp.float32), (clip_id[1:] == clip_id[:-1]).astype(jnp.float32)])
    factor = retain * continues[:, None]

    def advance(state_now, inputs_now):
        factor_now, driven_now = inputs_now
        state_now = factor_now[None, :] * state_now + driven_now
        return (state_now, state_now)
    final_state, states = lax.scan(advance, jnp.zeros((positions, model_width), jnp.float32), (factor, driven))
    output_rows = (states * out_gate).astype(jnp.bfloat16).reshape(-1, model_width)
    result = residual + grouped_product(output_rows, recur_out)
    return result.astype(jnp.bfloat16).reshape(frame_count, positions, model_width)
```

```python
import functools

import jax
import jax.numpy as jnp
from jax import lax
from jax.experimental import pallas as pl
from jax.experimental.pallas import tpu as pltpu
from jax.sharding import PartitionSpec as P

HEAD_DIMENSION = 64
WINDOW = 49
LONGEST_CLIP = 8
EPSILON = 1e-06

PAIR = 2 * WINDOW
BLOCK = 112
STEP_BLOCKS = 4
ROWS = 112

F32, BF16 = jnp.float32, jnp.bfloat16
VMEM_LIMIT = 60 * 1024 * 1024


def dot(a, b):
    return jnp.dot(a, b, preferred_element_type=F32)


def attend_kernel(place, x_ref, column_ref, row_ref, w_ref, own_ref, other_ref, normed, blended):
    step = pl.program_id(0)
    positions, width = x_ref.shape[1:]
    local = w_ref.shape[2]
    rows = STEP_BLOCKS * BLOCK

    @pl.when(step == 0)
    def _():
        @pl.loop(0, positions // ROWS)
        def _(i):
            at = pl.ds(pl.multiple_of(i * ROWS, ROWS), ROWS)
            x = x_ref[0, at, :].astype(F32)
            scale = lax.rsqrt(jnp.mean(x * x, axis=-1, keepdims=True) + EPSILON)
            normed[at, :] = (x * scale).astype(BF16)

    tokens = lax.broadcasted_iota(jnp.int32, (rows, positions), 1)
    pick = jnp.where(column_ref[...] == tokens, 1.0, 0.0).astype(BF16)
    gathered = dot(pick, normed[...]).astype(BF16)
    queries = (dot(gathered, w_ref[0]) * (HEAD_DIMENSION**-0.5)).astype(BF16)
    keys = dot(gathered, w_ref[1]).astype(BF16)
    values = dot(gathered, w_ref[2]).astype(BF16)

    two = 2 * HEAD_DIMENSION
    first = lax.broadcasted_iota(jnp.int32, (BLOCK, two), 1) < HEAD_DIMENSION
    row = lax.broadcasted_iota(jnp.int32, (2 * BLOCK, BLOCK), 0)
    row = jnp.where(row >= BLOCK, row - BLOCK, row)
    column = lax.broadcasted_iota(jnp.int32, (2 * BLOCK, BLOCK), 1)
    same = ((row < WINDOW) & (column < WINDOW)) | (
        (row >= WINDOW) & (column >= WINDOW) & (column < PAIR)
    )
    for block in range(STEP_BLOCKS):
        low = block * BLOCK
        for lane in range(0, local, two):
            q = queries[low : low + BLOCK, lane : lane + two]
            k = keys[low : low + BLOCK, lane : lane + two]
            v = values[low : low + BLOCK, lane : lane + two]
            none = jnp.zeros_like(q)
            both = jnp.concatenate([jnp.where(first, q, none), jnp.where(first, none, q)], axis=0)
            scores = lax.dot_general(
                both, k, (((1,), (1,)), ((), ())), preferred_element_type=F32
            )
            scores = jnp.where(same, scores, -1e30)
            raised = jnp.exp(scores - jnp.max(scores, axis=-1, keepdims=True))
            weights = raised * (1.0 / jnp.sum(raised, axis=-1, keepdims=True))
            mixed = dot(weights.astype(BF16), v)
            mixed = jnp.where(first, mixed[:BLOCK], mixed[BLOCK:]).astype(BF16)
            at = pl.ds(pl.multiple_of(step * rows + low, BLOCK), BLOCK)
            blended[at, lane : lane + two] = mixed

    @pl.when(step == pl.num_programs(0) - 1)
    def _():
        half = own_ref.shape[0]
        slots = blended.shape[0]
        for out_ref, side in ((own_ref, place[0]), (other_ref, 1 - place[0])):

            @pl.loop(0, half // ROWS)
            def _(i):
                token = lax.broadcasted_iota(jnp.int32, (ROWS, slots), 0) + (side * half + i * ROWS)
                put = jnp.where(token == row_ref[...], 1.0, 0.0).astype(BF16)
                at = pl.ds(pl.multiple_of(i * ROWS, ROWS), ROWS)
                out_ref[at, :] = dot(put, blended[...]).astype(BF16)


def attend(place, frame, video_tokens, order, weight):
    positions, width = video_tokens.shape[1:]
    local = weight.shape[2]
    slots = order.shape[0]
    rows = STEP_BLOCKS * BLOCK
    half = positions // 2
    once = pl.Buffered(1)
    return pl.pallas_call(
        attend_kernel,
        grid_spec=pltpu.PrefetchScalarGridSpec(
            num_scalar_prefetch=1,
            grid=(slots // rows,),
            in_specs=[
                pl.BlockSpec(
                    (1, positions, width), lambda i, s: (frame, 0, 0), pipeline_mode=once
                ),
                pl.BlockSpec((rows, 1), lambda i, s: (i, 0)),
                pl.BlockSpec((1, slots), lambda i, s: (0, 0), pipeline_mode=once),
                pl.BlockSpec((3, width, local), lambda i, s: (0, 0, 0), pipeline_mode=once),
            ],
            out_specs=[pl.BlockSpec((half, local), lambda i, s: (0, 0))] * 2,
            scratch_shapes=[
                pltpu.VMEM((positions, width), BF16),
                pltpu.VMEM((slots, local), BF16),
            ],
        ),
        out_shape=[jax.ShapeDtypeStruct((half, local), BF16)] * 2,
        compiler_params=pltpu.CompilerParams(vmem_limit_bytes=VMEM_LIMIT),
        cost_estimate=pl.CostEstimate(
            flops=2 * slots * width * (positions + 3 * local) + 2 * positions * slots * local,
            bytes_accessed=2 * (positions * (width + local) + 3 * width * local),
            transcendentals=slots * BLOCK * local // HEAD_DIMENSION,
        ),
        name="attend",
    )(place, video_tokens, order[:, None], order[None, :], weight)


def drive_kernel(frames, place, x_ref, *refs):
    own_refs, other_refs, refs = refs[:frames], refs[frames : 2 * frames], refs[2 * frames :]
    mix_own, mix_other, w_own, w_a, w_b, coef, factor = refs[:7]
    residual_ref, state_ref, gate_ref, low_ref, high_ref = refs[7:]
    width = x_ref.shape[2]
    own = jnp.concatenate([r[...] for r in own_refs], axis=0)
    other = jnp.concatenate([r[...] for r in other_refs], axis=0)
    mix = dot(own, mix_own[...]).astype(BF16).astype(F32)
    mix = mix + dot(other, mix_other[...]).astype(BF16).astype(F32)
    residual = x_ref[...].astype(F32).reshape(frames * ROWS, width) + mix
    residual_ref[...] = residual.reshape(frames, ROWS, width)
    scale = lax.rsqrt(jnp.mean(residual * residual, axis=-1, keepdims=True) + EPSILON)
    normed = (residual * scale).astype(BF16)
    low = 0
    for w in (w_own, w_a, w_b):
        high = low + w.shape[2]
        gate_in = jax.nn.sigmoid(dot(normed, w[0]))
        driven = gate_in * dot(normed, w[1])
        out = dot(normed, w[2])
        out = (out * jax.nn.sigmoid(out)).astype(BF16)
        state = None
        for f in range(frames):
            part = slice(f * ROWS, (f + 1) * ROWS)
            now = coef[f : f + 1, low:high] * driven[part]
            state = now if f == 0 else factor[f : f + 1, low:high] * state + now
            state_ref[f, :, low:high] = state.astype(BF16)
            gate_ref[f, :, low:high] = out[part]
        half = low_ref.shape[1]
        if high <= half:
            low_ref[:, low:high] = state.astype(BF16)
        else:
            high_ref[:, low - half : high - half] = state.astype(BF16)
        low = high


def drive(place, begin, count, video_tokens, own, other, weights, coef, factor):
    frames, positions, width = video_tokens.shape
    steps = positions // 2 // ROWS
    local = own[0].shape[1]
    once = pl.Buffered(1)

    def whole(array):
        zeros = (0,) * array.ndim
        return pl.BlockSpec(array.shape, lambda i, s: zeros, pipeline_mode=once)

    rows = count * ROWS
    constants = (*weights, coef, factor)
    wide = pl.BlockSpec((frames, ROWS, width), lambda i, s: (0, i, 0))
    narrow = pl.BlockSpec((ROWS, width // 2), lambda i, s: (i, 0))
    full = (frames, rows, width)
    return pl.pallas_call(
        functools.partial(drive_kernel, frames),
        grid_spec=pltpu.PrefetchScalarGridSpec(
            num_scalar_prefetch=1,
            grid=(count,),
            in_specs=[
                pl.BlockSpec((frames, ROWS, width), lambda i, s: (0, s[0] * steps + begin + i, 0))
            ]
            + [pl.BlockSpec((ROWS, local), lambda i, s: (begin + i, 0))] * (2 * frames)
            + [whole(c) for c in constants],
            out_specs=[wide, wide, wide, narrow, narrow],
        ),
        out_shape=[
            jax.ShapeDtypeStruct(full, F32),
            jax.ShapeDtypeStruct(full, BF16),
            jax.ShapeDtypeStruct(full, BF16),
            jax.ShapeDtypeStruct((rows, width // 2), BF16),
            jax.ShapeDtypeStruct((rows, width // 2), BF16),
        ],
        compiler_params=pltpu.CompilerParams(vmem_limit_bytes=VMEM_LIMIT),
        cost_estimate=pl.CostEstimate(
            flops=8 * frames * rows * width * width,
            bytes_accessed=frames * rows * width * 12 + 8 * width * width,
            transcendentals=2 * frames * rows * width,
        ),
        name="drive",
    )(place, video_tokens, *own, *other, *constants)


def emit_kernel(
    frames, place, low_ref, high_ref, state_ref, gate_ref, decay, res_keep, res_send, *refs
):
    kept, sent = refs[:3], refs[3:6]
    keep_ref, send_ref = refs[6:]
    half = low_ref.shape[1]
    incoming = (low_ref[...].astype(F32), high_ref[...].astype(F32))
    parts = []
    for side in range(2):
        lanes = slice(side * half, (side + 1) * half)
        rows = []
        for f in range(frames):
            state = state_ref[f, :, lanes].astype(F32) + decay[f : f + 1, lanes] * incoming[side]
            rows.append((state * gate_ref[f, :, lanes].astype(F32)).astype(BF16))
        parts.append(jnp.concatenate(rows, axis=0))
    for weights, residual, out in ((kept, res_keep, keep_ref), (sent, res_send, send_ref)):
        own, a, b = weights
        cut = a.shape[0]
        mix = dot(parts[0], own[...]).astype(BF16).astype(F32)
        rest = dot(parts[1][:, :cut], a[...]) + dot(parts[1][:, cut:], b[...])
        mix = mix + rest.astype(BF16).astype(F32)
        shape = residual.shape
        out[...] = (residual[...].reshape(mix.shape) + mix).astype(BF16).reshape(shape)


def emit(place, low, high, state, gate, decay, residual, weights):
    frames, rows, width = state.shape
    half = width // 2
    once = pl.Buffered(1)
    narrow = pl.BlockSpec((ROWS, half), lambda i, s: (i, 0))
    wide = pl.BlockSpec((frames, ROWS, width), lambda i, s: (0, i, 0))
    out = pl.BlockSpec((frames, ROWS, half), lambda i, s: (0, i, 0))

    def columns(array, mine):
        return pl.BlockSpec(
            (array.shape[0], half),
            lambda i, s: (0, s[0] if mine else 1 - s[0]),
            pipeline_mode=once,
        )

    return pl.pallas_call(
        functools.partial(emit_kernel, frames),
        grid_spec=pltpu.PrefetchScalarGridSpec(
            num_scalar_prefetch=1,
            grid=(rows // ROWS,),
            in_specs=[
                narrow,
                narrow,
                wide,
                wide,
                pl.BlockSpec(decay.shape, lambda i, s: (0, 0), pipeline_mode=once),
                pl.BlockSpec((frames, ROWS, half), lambda i, s: (0, i, s[0])),
                pl.BlockSpec((frames, ROWS, half), lambda i, s: (0, i, 1 - s[0])),
            ]
            + [columns(w, True) for w in weights]
            + [columns(w, False) for w in weights],
            out_specs=[out, out],
        ),
        out_shape=[jax.ShapeDtypeStruct((frames, rows, half), BF16)] * 2,
        compiler_params=pltpu.CompilerParams(vmem_limit_bytes=VMEM_LIMIT),
        cost_estimate=pl.CostEstimate(
            flops=2 * frames * rows * width * width,
            bytes_accessed=frames * rows * width * 12 + 2 * width * width,
            transcendentals=0,
        ),
        name="emit",
    )(place, low, high, state, gate, decay, residual, residual, *weights, *weights)


def swap(value, axis):
    count = lax.axis_size(axis)
    return lax.ppermute(value, axis, [(i, i ^ 1) for i in range(count)])


def shift(value, axis, steps):
    count = lax.axis_size(axis)
    return lax.ppermute(value, axis, [(i, i + steps) for i in range(count - steps)])


def fetch(value, dimension):
    size = value.shape[dimension] // 2
    start = lax.axis_index("clip") * size
    piece = swap(lax.dynamic_slice_in_dim(value, start, size, dimension), "head")
    return piece, swap(piece, "clip")


def incoming_state(low, high, decay, frames):
    odd = lax.axis_index("tm") % 2 == 1
    half = low.shape[1]
    decay_low, decay_high = decay[None, :half], decay[None, half:]
    sent = swap(jnp.where(odd, low, high), "tm")
    decay_sent = swap(jnp.where(odd, decay_low, decay_high), "tm")
    mine = jnp.where(odd, high, low).astype(F32)
    decay_mine = jnp.where(odd, decay_high, decay_low)
    sent = sent.astype(F32)
    earlier, later = jnp.where(odd, sent, mine), jnp.where(odd, mine, sent)
    decay_earlier = jnp.where(odd, decay_sent, decay_mine)
    decay_later = jnp.where(odd, decay_mine, decay_sent)
    both = decay_later * earlier + later
    decay_both = decay_later * decay_earlier
    entering = None if lax.axis_size("tm") > 2 else jnp.zeros_like(both)
    pairs = lax.axis_size("tm") // 2
    for _ in range(min(pairs - 1, -(-(LONGEST_CLIP - 1) // (2 * frames)))):
        total = both if entering is None else both + decay_both * entering
        entering = shift(total.astype(BF16), "tm", 2).astype(F32)
    second = earlier + decay_earlier * entering
    entering, second = entering.astype(BF16), second.astype(BF16)
    got = swap(jnp.where(odd, entering, second), "tm")
    return jnp.where(odd, got, entering), jnp.where(odd, second, got)


def per_device(
    video_tokens,
    window_order,
    clip_id,
    attend_weight,
    attend_out,
    recur_weight,
    frame_decay,
    recur_out,
):
    frames, positions, width = video_tokens.shape
    side = lax.axis_index("head")
    place = side.astype(jnp.int32).reshape(1)
    core = lax.axis_index("clip")

    out_a, out_b = fetch(attend_out, 0)
    mix_other = jnp.where(
        core == 0, jnp.concatenate([out_a, out_b], 0), jnp.concatenate([out_b, out_a], 0)
    )
    decay_other = swap(frame_decay, "head")
    cut = decay_other.shape[1] // 2
    decay_a, decay_b = decay_other[:, :cut], decay_other[:, cut:]
    frame_decay = jnp.concatenate(
        [
            frame_decay,
            jnp.where(core == 0, decay_a, decay_b),
            jnp.where(core == 0, decay_b, decay_a),
        ],
        axis=1,
    )
    recur_a, recur_b = fetch(recur_weight, 2)
    emit_a, emit_b = fetch(recur_out, 0)

    retain = jnp.exp(frame_decay)
    coef = jnp.sqrt(1.0 - retain * retain)
    previous = shift(clip_id[frames - 1 :], "tm", 1)
    continues = (clip_id == jnp.concatenate([previous, clip_id[:-1]])).astype(F32)
    factor = retain * continues[:, None]
    decay_all = jnp.cumprod(factor, axis=0)

    order = window_order.reshape(frames, positions // PAIR, PAIR)
    order = jnp.pad(order, ((0, 0), (0, 0), (0, BLOCK - PAIR)), constant_values=-1)
    order = order.reshape(frames, -1)
    own, other = [], []
    for f in range(frames):
        mine, theirs = attend(place, f, video_tokens, order[f], attend_weight)
        own.append(mine)
        other.append(swap(theirs, "head"))

    weights = (attend_out, mix_other, recur_weight, recur_a, recur_b)
    steps = positions // 2 // ROWS
    cuts = [0, (steps + 1) // 2, steps]
    driven = [
        drive(place, begin, end - begin, video_tokens, own, other, weights, coef, factor)
        for begin, end in zip(cuts, cuts[1:])
    ]
    kept, received = [], []
    for residual, state, gate, low, high in driven:
        low, high = incoming_state(low, high, decay_all[-1], frames)
        keep, send = emit(
            place, low, high, state, gate, decay_all, residual, (recur_out, emit_a, emit_b)
        )
        kept.append(keep)
        received.append(swap(send, "head"))
    return jnp.where(
        side == 0,
        jnp.concatenate(kept + received, axis=1),
        jnp.concatenate(received + kept, axis=1),
    )


def from_behind(value, axis, steps):
    count = lax.axis_size(axis)
    leading, last = (max(0, -steps), min(count, count - steps))
    return lax.ppermute(value, axis, [(source, source + steps) for source in range(leading, last)])


def prefix_2(value, axis, combine, identity):
    count, position = (lax.axis_size(axis), lax.axis_index(axis))
    everything = jax.tree.map(
        lambda part, kind: lax.all_gather(part.astype(kind), axis),
        value,
        (jnp.bfloat16, jnp.bfloat16),
    )
    start = jax.tree.map(
        lambda part, zero: jnp.broadcast_to(jnp.asarray(zero, part.dtype), part.shape),
        value,
        identity,
    )

    def hop(k, before):
        reached = k < position
        new = combine(
            before, jax.tree.map(lambda part, own: part[k].astype(own.dtype), everything, value)
        )
        return jax.tree.map(lambda a, b: jnp.where(reached, a, b), new, before)

    return lax.fori_loop(0, count, hop, start)


def normalize(values):
    return values * lax.rsqrt(jnp.mean(values * values, axis=-1, keepdims=True) + EPSILON)


def window_attention(queries, keys_all, values_all, window_order):
    frame_count, positions, number_of_heads, head_size = queries.shape
    order_index = window_order[:, :, None, None]

    def arrange(tensor):
        reordered = jnp.take_along_axis(tensor, order_index, axis=1)
        return reordered.reshape(
            frame_count, positions // WINDOW, WINDOW, number_of_heads, head_size
        )

    scores = jnp.einsum(
        "fwihe,fwjhe->fwhij",
        arrange(queries),
        arrange(keys_all),
        preferred_element_type=jnp.float32,
    ) / jnp.sqrt(jnp.float32(head_size))
    weights = jax.nn.softmax(scores, axis=-1).astype(jnp.bfloat16)
    blended = jnp.einsum(
        "fwhij,fwjhe->fwihe", weights, arrange(values_all), preferred_element_type=jnp.float32
    ).astype(jnp.bfloat16)
    blended = blended.reshape(frame_count, positions, number_of_heads, head_size)
    inverse = jnp.argsort(window_order, axis=1)
    return jnp.take_along_axis(blended, inverse[:, :, None, None], axis=1)


def per_device_any(
    video_tokens,
    window_order,
    clip_id,
    attend_weight,
    attend_out,
    recur_weight,
    frame_decay,
    recur_out,
):
    frame_count, positions, model_width = video_tokens.shape
    local_width = attend_weight.shape[2]
    row_count = frame_count * positions
    inputs = video_tokens.reshape(row_count, model_width).astype(jnp.float32)
    normed = normalize(inputs).astype(jnp.bfloat16)
    projected = jnp.einsum(
        "td,kde->kte", normed, attend_weight, preferred_element_type=jnp.float32
    ).astype(jnp.bfloat16)
    shaped = projected.reshape(
        3, frame_count, positions, local_width // HEAD_DIMENSION, HEAD_DIMENSION
    )
    attended = window_attention(shaped[0], shaped[1], shaped[2], window_order).reshape(
        row_count, local_width
    )
    partial_mix = jnp.dot(attended, attend_out, preferred_element_type=jnp.float32)
    offset = lax.axis_index("head") * local_width
    residual = inputs + lax.psum(partial_mix.astype(jnp.bfloat16), "head").astype(jnp.float32)
    normed_again = normalize(residual).astype(jnp.bfloat16)
    recur_proj = jnp.einsum(
        "td,kde->kte", normed_again, recur_weight, preferred_element_type=jnp.float32
    )
    residual_own = lax.dynamic_slice_in_dim(residual, offset, local_width, 1)
    gate_in = jax.nn.sigmoid(recur_proj[0]).reshape(frame_count, positions, local_width)
    value_in = recur_proj[1].reshape(frame_count, positions, local_width)
    out_gate = jax.nn.silu(recur_proj[2]).reshape(frame_count, positions, local_width)
    retain = jnp.exp(frame_decay)
    driven = jnp.sqrt(1.0 - retain * retain)[:, None, :] * gate_in * value_in
    previous = from_behind(clip_id[frame_count - 1 :], "tm", 1)
    continues = jnp.concatenate(
        [
            (clip_id[:1] == previous).astype(jnp.float32),
            (clip_id[1:] == clip_id[:-1]).astype(jnp.float32),
        ]
    )
    factor = retain * continues[:, None]

    def advance(carried, inputs_now):
        decay_total, state_now = carried
        factor_now, driven_now = inputs_now
        decay_total = factor_now * decay_total
        state_now = factor_now[None, :] * state_now + driven_now
        return ((decay_total, state_now), (decay_total, state_now))

    start_carry = (
        jnp.ones((local_width,), jnp.float32),
        jnp.zeros((positions, local_width), jnp.float32),
    )
    last_carry, all_carry = lax.scan(advance, start_carry, (factor, driven))
    decay_last, state_last = last_carry
    decay_all, state_all = all_carry

    def combine(earlier, later_part):
        return (later_part[0] * earlier[0], later_part[0][None, :] * earlier[1] + later_part[1])

    prefix = prefix_2(
        (decay_last, state_last),
        "tm",
        combine,
        (jnp.ones_like(decay_last), jnp.zeros_like(state_last)),
    )
    incoming = prefix[1]
    states = state_all + decay_all[:, None, :] * incoming[None, :, :]
    output_rows = (states * out_gate).astype(jnp.bfloat16).reshape(row_count, local_width)
    partial_out = jnp.dot(output_rows, recur_out, preferred_element_type=jnp.float32)
    result = residual_own + lax.psum_scatter(
        partial_out.astype(jnp.bfloat16), "head", scatter_dimension=1, tiled=True
    ).astype(jnp.float32)
    return result.astype(jnp.bfloat16).reshape(frame_count, positions, local_width)


def solution(mesh):
    halves = mesh.shape["head"] == 2 and mesh.shape["clip"] == 2 and mesh.shape["tm"] % 2 == 0
    return jax.shard_map(
        per_device if halves else per_device_any,
        mesh=mesh,
        in_specs=(
            P(("clip", "tm"), None, None),
            P(("clip", "tm"), None),
            P(("clip", "tm")),
            P(None, None, "head"),
            P("head", None),
            P(None, None, "head"),
            P(("clip", "tm"), "head"),
            P("head", None),
        ),
        out_specs=P(("clip", "tm"), None, "head"),
        check_vma=False,
    )
```

```python
import functools

import jax
import jax.numpy as jnp
from jax import lax
from jax.experimental import pallas as pl
from jax.experimental.pallas import tpu as pltpu
from jax.sharding import PartitionSpec as P

HEAD_DIMENSION = 64
WINDOW = 49
LONGEST_CLIP = 8
EPSILON = 1e-06

PAIR = 2 * WINDOW
BLOCK = 112
STEP_BLOCKS = 4
ROWS = 112

F32, BF16 = jnp.float32, jnp.bfloat16
VMEM_LIMIT = 58 * 1024 * 1024
SMALL_LIMIT = 24 * 1024 * 1024
SHARES = (4, 3)


def dot(a, b):
    return jnp.dot(a, b, preferred_element_type=F32)


def attend_kernel(place, x_ref, column_ref, row_ref, w_ref, own_ref, other_ref, normed, blended):
    step = pl.program_id(0)
    positions, width = x_ref.shape[1:]
    local = w_ref.shape[2]
    rows = STEP_BLOCKS * BLOCK

    @pl.when(step == 0)
    def _():
        @pl.loop(0, positions // ROWS)
        def _(i):
            at = pl.ds(pl.multiple_of(i * ROWS, ROWS), ROWS)
            x = x_ref[0, at, :].astype(F32)
            scale = lax.rsqrt(jnp.mean(x * x, axis=-1, keepdims=True) + EPSILON)
            normed[at, :] = (x * scale).astype(BF16)

    tokens = lax.broadcasted_iota(jnp.int32, (rows, positions), 1)
    pick = jnp.where(column_ref[...] == tokens, 1.0, 0.0).astype(BF16)
    gathered = dot(pick, normed[...]).astype(BF16)
    queries = (dot(gathered, w_ref[0]) * (HEAD_DIMENSION**-0.5)).astype(BF16)
    keys = dot(gathered, w_ref[1]).astype(BF16)
    values = dot(gathered, w_ref[2]).astype(BF16)

    two = 2 * HEAD_DIMENSION
    first = lax.broadcasted_iota(jnp.int32, (BLOCK, two), 1) < HEAD_DIMENSION
    row = lax.broadcasted_iota(jnp.int32, (2 * BLOCK, BLOCK), 0)
    row = jnp.where(row >= BLOCK, row - BLOCK, row)
    column = lax.broadcasted_iota(jnp.int32, (2 * BLOCK, BLOCK), 1)
    same = ((row < WINDOW) & (column < WINDOW)) | (
        (row >= WINDOW) & (column >= WINDOW) & (column < PAIR)
    )
    for block in range(STEP_BLOCKS):
        low = block * BLOCK
        for lane in range(0, local, two):
            q = queries[low : low + BLOCK, lane : lane + two]
            k = keys[low : low + BLOCK, lane : lane + two]
            v = values[low : low + BLOCK, lane : lane + two]
            none = jnp.zeros_like(q)
            both = jnp.concatenate([jnp.where(first, q, none), jnp.where(first, none, q)], axis=0)
            scores = lax.dot_general(
                both, k, (((1,), (1,)), ((), ())), preferred_element_type=F32
            )
            scores = jnp.where(same, scores, -1e30)
            raised = jnp.exp(scores - jnp.max(scores, axis=-1, keepdims=True))
            weights = raised * (1.0 / jnp.sum(raised, axis=-1, keepdims=True))
            mixed = dot(weights.astype(BF16), v)
            mixed = jnp.where(first, mixed[:BLOCK], mixed[BLOCK:]).astype(BF16)
            at = pl.ds(pl.multiple_of(step * rows + low, BLOCK), BLOCK)
            blended[at, lane : lane + two] = mixed

    @pl.when(step == pl.num_programs(0) - 1)
    def _():
        half = own_ref.shape[0]
        slots = blended.shape[0]
        for out_ref, side in ((own_ref, place[0]), (other_ref, 1 - place[0])):

            @pl.loop(0, half // ROWS)
            def _(i):
                token = lax.broadcasted_iota(jnp.int32, (ROWS, slots), 0) + (side * half + i * ROWS)
                put = jnp.where(token == row_ref[...], 1.0, 0.0).astype(BF16)
                at = pl.ds(pl.multiple_of(i * ROWS, ROWS), ROWS)
                out_ref[at, :] = dot(put, blended[...]).astype(BF16)


def attend(place, frame, video_tokens, order, weight):
    positions, width = video_tokens.shape[1:]
    local = weight.shape[2]
    slots = order.shape[0]
    rows = STEP_BLOCKS * BLOCK
    half = positions // 2
    once = pl.Buffered(1)
    return pl.pallas_call(
        attend_kernel,
        grid_spec=pltpu.PrefetchScalarGridSpec(
            num_scalar_prefetch=1,
            grid=(slots // rows,),
            in_specs=[
                pl.BlockSpec(
                    (1, positions, width), lambda i, s: (frame, 0, 0), pipeline_mode=once
                ),
                pl.BlockSpec((rows, 1), lambda i, s: (i, 0)),
                pl.BlockSpec((1, slots), lambda i, s: (0, 0), pipeline_mode=once),
                pl.BlockSpec((3, width, local), lambda i, s: (0, 0, 0), pipeline_mode=once),
            ],
            out_specs=[pl.BlockSpec((half, local), lambda i, s: (0, 0))] * 2,
            scratch_shapes=[
                pltpu.VMEM((positions, width), BF16),
                pltpu.VMEM((slots, local), BF16),
            ],
        ),
        out_shape=[jax.ShapeDtypeStruct((half, local), BF16)] * 2,
        compiler_params=pltpu.CompilerParams(vmem_limit_bytes=VMEM_LIMIT),
        cost_estimate=pl.CostEstimate(
            flops=2 * slots * width * (positions + 3 * local) + 2 * positions * slots * local,
            bytes_accessed=2 * (positions * (width + local) + 3 * width * local),
            transcendentals=slots * BLOCK * local // HEAD_DIMENSION,
        ),
        name="attend",
    )(place, video_tokens, order[:, None], order[None, :], weight)


def drive_kernel(follows, place, x_ref, own_ref, other_ref, *refs):
    mix_own, mix_other, w_own, w_a, w_b, coef, factor = refs[:7]
    before, refs = (refs[7:9], refs[9:]) if follows else (None, refs[7:])
    residual_ref, gate_ref, low_ref, high_ref = refs
    mix = dot(own_ref[...], mix_own[...]).astype(BF16).astype(F32)
    mix = mix + dot(other_ref[...], mix_other[...]).astype(BF16).astype(F32)
    residual = x_ref[0].astype(F32) + mix
    residual_ref[...] = residual
    scale = lax.rsqrt(jnp.mean(residual * residual, axis=-1, keepdims=True) + EPSILON)
    normed = (residual * scale).astype(BF16)
    low, half = 0, low_ref.shape[1]
    for w in (w_own, w_a, w_b):
        high = low + w.shape[2]
        gate_in = jax.nn.sigmoid(dot(normed, w[0]))
        state = coef[:, low:high] * gate_in * dot(normed, w[1])
        out = dot(normed, w[2])
        gate_ref[:, low:high] = (out * jax.nn.sigmoid(out)).astype(BF16)
        side = int(high > half)
        lanes = slice(low - side * half, high - side * half)
        if follows:
            state = state + factor[:, low:high] * before[side][:, lanes].astype(F32)
        (low_ref, high_ref)[side][:, lanes] = state.astype(BF16)
        low = high


def held():
    return pl.BlockSpec(memory_space=pltpu.VMEM)


def drive(place, frame, begin, count, video_tokens, own, other, weights, coef, factor, before):
    positions, width = video_tokens.shape[1:]
    steps = positions // 2 // ROWS
    local = own.shape[1]
    rows, half = count * ROWS, width // 2
    later = pl.BlockSpec((ROWS, half), lambda i, s: (begin + i, 0))
    wide = pl.BlockSpec((ROWS, width), lambda i, s: (i, 0))
    narrow = pl.BlockSpec((ROWS, half), lambda i, s: (i, 0))
    return pl.pallas_call(
        functools.partial(drive_kernel, before is not None),
        grid_spec=pltpu.PrefetchScalarGridSpec(
            num_scalar_prefetch=1,
            grid=(count,),
            in_specs=[
                pl.BlockSpec((1, ROWS, width), lambda i, s: (frame, s[0] * steps + begin + i, 0))
            ]
            + [pl.BlockSpec((ROWS, local), lambda i, s: (begin + i, 0))] * 2
            + [held()] * (len(weights) + 2)
            + [later] * (0 if before is None else 2),
            out_specs=[wide, wide, narrow, narrow],
        ),
        out_shape=[
            jax.ShapeDtypeStruct((rows, width), F32),
            jax.ShapeDtypeStruct((rows, width), BF16),
            jax.ShapeDtypeStruct((rows, half), BF16),
            jax.ShapeDtypeStruct((rows, half), BF16),
        ],
        compiler_params=pltpu.CompilerParams(vmem_limit_bytes=SMALL_LIMIT),
        cost_estimate=pl.CostEstimate(
            flops=8 * rows * width * width,
            bytes_accessed=rows * width * 12,
            transcendentals=2 * rows * width,
        ),
        name="drive",
    )(
        place,
        video_tokens,
        own,
        other,
        *weights,
        coef[frame : frame + 1],
        factor[frame : frame + 1],
        *(() if before is None else before),
    )


def emit_kernel(frames, place, low_ref, high_ref, decay, own, a, b, *refs):
    each, (keep_ref, send_ref) = refs[: 5 * frames], refs[-2:]
    half = low_ref.shape[1]
    incoming = (low_ref[...].astype(F32), high_ref[...].astype(F32))
    parts = [[], []]
    for f in range(frames):
        gate = each[5 * f + 2]
        for side in range(2):
            lanes = slice(side * half, (side + 1) * half)
            state = each[5 * f + side][...].astype(F32)
            state = state + decay[f : f + 1, lanes] * incoming[side]
            parts[side].append((state * gate[:, lanes].astype(F32)).astype(BF16))
    first, second = (jnp.concatenate(p, axis=0) for p in parts)
    cut = a.shape[0]
    for which, out in ((0, keep_ref), (1, send_ref)):
        side = 1 - place[0] if which else place[0]
        lanes = pl.ds(pl.multiple_of(side * half, half), half)
        mix = dot(first, own[:, lanes]).astype(BF16).astype(F32)
        rest = dot(second[:, :cut], a[:, lanes]) + dot(second[:, cut:], b[:, lanes])
        mix = mix + rest.astype(BF16).astype(F32)
        for f in range(frames):
            residual = each[5 * f + 3 + which][...]
            out[f] = (residual + mix[f * ROWS : (f + 1) * ROWS]).astype(BF16)


def emit(place, begin, total, low, high, decay, weights, states, result):
    frames, (rows, half) = len(states), low.shape
    narrow = pl.BlockSpec((ROWS, half), lambda i, s: (i, 0))
    out = pl.BlockSpec((frames, ROWS, half), lambda i, s: (0, i, 0))
    steps = total // 2 // ROWS
    placed = pl.BlockSpec((frames, ROWS, half), lambda i, s: (0, s[0] * steps + begin + i, 0))
    specs, arrays, aliases = [], [], {}
    for f, (residual, gate, low_f, high_f) in enumerate(states):
        at = 0 if f == frames - 1 else begin
        specs += [pl.BlockSpec((ROWS, half), lambda i, s, at=at: (at + i, 0))] * 2
        specs += [
            pl.BlockSpec((ROWS, 2 * half), lambda i, s, at=at: (at + i, 0)),
            pl.BlockSpec((ROWS, half), lambda i, s, at=at: (at + i, s[0])),
            pl.BlockSpec((ROWS, half), lambda i, s, at=at: (at + i, 1 - s[0])),
        ]
        arrays += [low_f, high_f, gate, residual, residual]
    if result is not None:
        aliases = {7 + len(arrays): 0}
        specs.append(pl.BlockSpec(memory_space=pl.ANY))
        arrays.append(result)
    return pl.pallas_call(
        functools.partial(emit_kernel, frames),
        grid_spec=pltpu.PrefetchScalarGridSpec(
            num_scalar_prefetch=1,
            grid=(rows // ROWS,),
            in_specs=[narrow, narrow] + [held()] * 4 + specs,
            out_specs=[placed, out],
        ),
        out_shape=[
            jax.ShapeDtypeStruct((frames, total, half), BF16),
            jax.ShapeDtypeStruct((frames, rows, half), BF16),
        ],
        input_output_aliases=aliases,
        compiler_params=pltpu.CompilerParams(vmem_limit_bytes=SMALL_LIMIT),
        cost_estimate=pl.CostEstimate(
            flops=8 * frames * rows * half * half,
            bytes_accessed=frames * rows * half * 24,
            transcendentals=0,
        ),
        name="emit",
    )(place, low, high, decay, *weights, *arrays)


def swap(value, axis):
    count = lax.axis_size(axis)
    return lax.ppermute(value, axis, [(i, i ^ 1) for i in range(count)])


def shift(value, axis, steps):
    count = lax.axis_size(axis)
    return lax.ppermute(value, axis, [(i, i + steps) for i in range(count - steps)])


def fetch(value, dimension):
    size = value.shape[dimension] // 2
    start = lax.axis_index("clip") * size
    piece = swap(lax.dynamic_slice_in_dim(value, start, size, dimension), "head")
    return piece, swap(piece, "clip")


def incoming_state(low, high, decay, frames):
    odd = lax.axis_index("tm") % 2 == 1
    half = low.shape[1]
    decay_low, decay_high = decay[None, :half], decay[None, half:]
    sent = swap(jnp.where(odd, low, high), "tm")
    decay_sent = swap(jnp.where(odd, decay_low, decay_high), "tm")
    mine = jnp.where(odd, high, low).astype(F32)
    decay_mine = jnp.where(odd, decay_high, decay_low)
    sent = sent.astype(F32)
    earlier, later = jnp.where(odd, sent, mine), jnp.where(odd, mine, sent)
    decay_earlier = jnp.where(odd, decay_sent, decay_mine)
    decay_later = jnp.where(odd, decay_mine, decay_sent)
    both = decay_later * earlier + later
    decay_both = decay_later * decay_earlier
    entering = None if lax.axis_size("tm") > 2 else jnp.zeros_like(both)
    pairs = lax.axis_size("tm") // 2
    for _ in range(min(pairs - 1, -(-(LONGEST_CLIP - 1) // (2 * frames)))):
        total = both if entering is None else both + decay_both * entering
        entering = shift(total.astype(BF16), "tm", 2).astype(F32)
    second = earlier + decay_earlier * entering
    entering, second = entering.astype(BF16), second.astype(BF16)
    got = swap(jnp.where(odd, entering, second), "tm")
    return jnp.where(odd, got, entering), jnp.where(odd, second, got)


def per_device(
    video_tokens,
    window_order,
    clip_id,
    attend_weight,
    attend_out,
    recur_weight,
    frame_decay,
    recur_out,
):
    frames, positions, width = video_tokens.shape
    side = lax.axis_index("head")
    place = side.astype(jnp.int32).reshape(1)
    core = lax.axis_index("clip")

    out_a, out_b = fetch(attend_out, 0)
    mix_other = jnp.where(
        core == 0, jnp.concatenate([out_a, out_b], 0), jnp.concatenate([out_b, out_a], 0)
    )
    decay_other = swap(frame_decay, "head")
    cut = decay_other.shape[1] // 2
    decay_a, decay_b = decay_other[:, :cut], decay_other[:, cut:]
    frame_decay = jnp.concatenate(
        [
            frame_decay,
            jnp.where(core == 0, decay_a, decay_b),
            jnp.where(core == 0, decay_b, decay_a),
        ],
        axis=1,
    )
    recur_a, recur_b = fetch(recur_weight, 2)
    emit_a, emit_b = fetch(recur_out, 0)

    retain = jnp.exp(frame_decay)
    coef = jnp.sqrt(1.0 - retain * retain)
    previous = shift(clip_id[frames - 1 :], "tm", 1)
    continues = (clip_id == jnp.concatenate([previous, clip_id[:-1]])).astype(F32)
    factor = retain * continues[:, None]
    decay_all = jnp.cumprod(factor, axis=0)

    order = window_order.reshape(frames, positions // PAIR, PAIR)
    order = jnp.pad(order, ((0, 0), (0, 0), (0, BLOCK - PAIR)), constant_values=-1)
    order = order.reshape(frames, -1)
    weights = (attend_out, mix_other, recur_weight, recur_a, recur_b)
    own, other = [], []
    for f in range(frames):
        placed = order[f]
        if f:
            placed, coef, factor, out_a = lax.optimization_barrier((placed, coef, factor, out_a))
        mine, theirs = attend(place, f, video_tokens, placed, attend_weight)
        own.append(mine)
        other.append(swap(theirs, "head"))

    steps = positions // 2 // ROWS
    cuts = [steps * sum(SHARES[:k]) // sum(SHARES) for k in range(len(SHARES) + 1)]
    states = []
    for f in range(frames - 1):
        before = states[-1][2:] if states else None
        states.append(
            drive(
                place, f, 0, steps, video_tokens, own[f], other[f], weights, coef, factor, before
            )
        )
    before = states[-1][2:] if states else None
    result, received = None, []
    for begin, end in zip(cuts, cuts[1:]):
        f = frames - 1
        last = drive(
            place,
            f,
            begin,
            end - begin,
            video_tokens,
            own[f],
            other[f],
            weights,
            coef,
            factor,
            before,
        )
        low, high = incoming_state(last[2], last[3], decay_all[-1], frames)
        result, send = emit(
            place,
            begin,
            positions,
            low,
            high,
            decay_all,
            (recur_out, emit_a, emit_b),
            [*states, last],
            result,
        )
        received.append(swap(send, "head"))
    for begin, part in zip(cuts, received):
        at = (1 - side) * (positions // 2) + begin * ROWS
        result = lax.dynamic_update_slice_in_dim(result, part, at, 1)
    return result


def from_behind(value, axis, steps):
    count = lax.axis_size(axis)
    leading, last = (max(0, -steps), min(count, count - steps))
    return lax.ppermute(value, axis, [(source, source + steps) for source in range(leading, last)])


def prefix_2(value, axis, combine, identity):
    count, position = (lax.axis_size(axis), lax.axis_index(axis))
    everything = jax.tree.map(
        lambda part, kind: lax.all_gather(part.astype(kind), axis),
        value,
        (jnp.bfloat16, jnp.bfloat16),
    )
    start = jax.tree.map(
        lambda part, zero: jnp.broadcast_to(jnp.asarray(zero, part.dtype), part.shape),
        value,
        identity,
    )

    def hop(k, before):
        reached = k < position
        new = combine(
            before, jax.tree.map(lambda part, own: part[k].astype(own.dtype), everything, value)
        )
        return jax.tree.map(lambda a, b: jnp.where(reached, a, b), new, before)

    return lax.fori_loop(0, count, hop, start)


def normalize(values):
    return values * lax.rsqrt(jnp.mean(values * values, axis=-1, keepdims=True) + EPSILON)


def window_attention(queries, keys_all, values_all, window_order):
    frame_count, positions, number_of_heads, head_size = queries.shape
    order_index = window_order[:, :, None, None]

    def arrange(tensor):
        reordered = jnp.take_along_axis(tensor, order_index, axis=1)
        return reordered.reshape(
            frame_count, positions // WINDOW, WINDOW, number_of_heads, head_size
        )

    scores = jnp.einsum(
        "fwihe,fwjhe->fwhij",
        arrange(queries),
        arrange(keys_all),
        preferred_element_type=jnp.float32,
    ) / jnp.sqrt(jnp.float32(head_size))
    weights = jax.nn.softmax(scores, axis=-1).astype(jnp.bfloat16)
    blended = jnp.einsum(
        "fwhij,fwjhe->fwihe", weights, arrange(values_all), preferred_element_type=jnp.float32
    ).astype(jnp.bfloat16)
    blended = blended.reshape(frame_count, positions, number_of_heads, head_size)
    inverse = jnp.argsort(window_order, axis=1)
    return jnp.take_along_axis(blended, inverse[:, :, None, None], axis=1)


def per_device_any(
    video_tokens,
    window_order,
    clip_id,
    attend_weight,
    attend_out,
    recur_weight,
    frame_decay,
    recur_out,
):
    frame_count, positions, model_width = video_tokens.shape
    local_width = attend_weight.shape[2]
    row_count = frame_count * positions
    inputs = video_tokens.reshape(row_count, model_width).astype(jnp.float32)
    normed = normalize(inputs).astype(jnp.bfloat16)
    projected = jnp.einsum(
        "td,kde->kte", normed, attend_weight, preferred_element_type=jnp.float32
    ).astype(jnp.bfloat16)
    shaped = projected.reshape(
        3, frame_count, positions, local_width // HEAD_DIMENSION, HEAD_DIMENSION
    )
    attended = window_attention(shaped[0], shaped[1], shaped[2], window_order).reshape(
        row_count, local_width
    )
    partial_mix = jnp.dot(attended, attend_out, preferred_element_type=jnp.float32)
    offset = lax.axis_index("head") * local_width
    residual = inputs + lax.psum(partial_mix.astype(jnp.bfloat16), "head").astype(jnp.float32)
    normed_again = normalize(residual).astype(jnp.bfloat16)
    recur_proj = jnp.einsum(
        "td,kde->kte", normed_again, recur_weight, preferred_element_type=jnp.float32
    )
    residual_own = lax.dynamic_slice_in_dim(residual, offset, local_width, 1)
    gate_in = jax.nn.sigmoid(recur_proj[0]).reshape(frame_count, positions, local_width)
    value_in = recur_proj[1].reshape(frame_count, positions, local_width)
    out_gate = jax.nn.silu(recur_proj[2]).reshape(frame_count, positions, local_width)
    retain = jnp.exp(frame_decay)
    driven = jnp.sqrt(1.0 - retain * retain)[:, None, :] * gate_in * value_in
    previous = from_behind(clip_id[frame_count - 1 :], "tm", 1)
    continues = jnp.concatenate(
        [
            (clip_id[:1] == previous).astype(jnp.float32),
            (clip_id[1:] == clip_id[:-1]).astype(jnp.float32),
        ]
    )
    factor = retain * continues[:, None]

    def advance(carried, inputs_now):
        decay_total, state_now = carried
        factor_now, driven_now = inputs_now
        decay_total = factor_now * decay_total
        state_now = factor_now[None, :] * state_now + driven_now
        return ((decay_total, state_now), (decay_total, state_now))

    start_carry = (
        jnp.ones((local_width,), jnp.float32),
        jnp.zeros((positions, local_width), jnp.float32),
    )
    last_carry, all_carry = lax.scan(advance, start_carry, (factor, driven))
    decay_last, state_last = last_carry
    decay_all, state_all = all_carry

    def combine(earlier, later_part):
        return (later_part[0] * earlier[0], later_part[0][None, :] * earlier[1] + later_part[1])

    prefix = prefix_2(
        (decay_last, state_last),
        "tm",
        combine,
        (jnp.ones_like(decay_last), jnp.zeros_like(state_last)),
    )
    incoming = prefix[1]
    states = state_all + decay_all[:, None, :] * incoming[None, :, :]
    output_rows = (states * out_gate).astype(jnp.bfloat16).reshape(row_count, local_width)
    partial_out = jnp.dot(output_rows, recur_out, preferred_element_type=jnp.float32)
    result = residual_own + lax.psum_scatter(
        partial_out.astype(jnp.bfloat16), "head", scatter_dimension=1, tiled=True
    ).astype(jnp.float32)
    return result.astype(jnp.bfloat16).reshape(frame_count, positions, local_width)


def solution(mesh):
    halves = mesh.shape["head"] == 2 and mesh.shape["clip"] == 2 and mesh.shape["tm"] % 2 == 0
    return jax.shard_map(
        per_device if halves else per_device_any,
        mesh=mesh,
        in_specs=(
            P(("clip", "tm"), None, None),
            P(("clip", "tm"), None),
            P(("clip", "tm")),
            P(None, None, "head"),
            P("head", None),
            P(None, None, "head"),
            P(("clip", "tm"), "head"),
            P("head", None),
        ),
        out_specs=P(("clip", "tm"), None, "head"),
        check_vma=False,
    )
```

```python
import functools

import jax
import jax.numpy as jnp
from jax import lax
from jax.experimental import pallas as pl
from jax.experimental.pallas import tpu as pltpu
from jax.sharding import PartitionSpec as P

HEAD_DIMENSION = 64
WINDOW = 49
LONGEST_CLIP = 8
EPSILON = 1e-06

PAIR = 2 * WINDOW
BLOCK = 112
STEP_BLOCKS = 8
ROWS = 112

F32, BF16 = jnp.float32, jnp.bfloat16
VMEM_LIMIT = 58 * 1024 * 1024
SMALL_LIMIT = 24 * 1024 * 1024
SHARES = (4, 3)


def dot(a, b):
    return jnp.dot(a, b, preferred_element_type=F32)


def attend_kernel(place, x_ref, column_ref, row_ref, w_ref, own_ref, other_ref, normed, blended):
    step = pl.program_id(0)
    positions, width = x_ref.shape[1:]
    local = w_ref.shape[2]
    rows = STEP_BLOCKS * BLOCK

    @pl.when(step == 0)
    def _():
        @pl.loop(0, positions // ROWS)
        def _(i):
            at = pl.ds(pl.multiple_of(i * ROWS, ROWS), ROWS)
            x = x_ref[0, at, :].astype(F32)
            scale = lax.rsqrt(jnp.mean(x * x, axis=-1, keepdims=True) + EPSILON)
            normed[at, :] = (x * scale).astype(BF16)

    tokens = lax.broadcasted_iota(jnp.int32, (rows, positions), 1)
    pick = jnp.where(column_ref[...] == tokens, 1.0, 0.0).astype(BF16)
    gathered = dot(pick, normed[...]).astype(BF16)
    queries = (dot(gathered, w_ref[0]) * (HEAD_DIMENSION**-0.5)).astype(BF16)
    keys = dot(gathered, w_ref[1]).astype(BF16)
    values = dot(gathered, w_ref[2]).astype(BF16)

    two = 2 * HEAD_DIMENSION
    first = lax.broadcasted_iota(jnp.int32, (BLOCK, two), 1) < HEAD_DIMENSION
    row = lax.broadcasted_iota(jnp.int32, (2 * BLOCK, BLOCK), 0)
    row = jnp.where(row >= BLOCK, row - BLOCK, row)
    column = lax.broadcasted_iota(jnp.int32, (2 * BLOCK, BLOCK), 1)
    same = ((row < WINDOW) & (column < WINDOW)) | (
        (row >= WINDOW) & (column >= WINDOW) & (column < PAIR)
    )
    for block in range(STEP_BLOCKS):
        low = block * BLOCK
        for lane in range(0, local, two):
            q = queries[low : low + BLOCK, lane : lane + two]
            k = keys[low : low + BLOCK, lane : lane + two]
            v = values[low : low + BLOCK, lane : lane + two]
            none = jnp.zeros_like(q)
            both = jnp.concatenate([jnp.where(first, q, none), jnp.where(first, none, q)], axis=0)
            scores = lax.dot_general(
                both, k, (((1,), (1,)), ((), ())), preferred_element_type=F32
            )
            scores = jnp.where(same, scores, -1e30)
            raised = jnp.exp(scores - jnp.max(scores, axis=-1, keepdims=True))
            weights = raised * (1.0 / jnp.sum(raised, axis=-1, keepdims=True))
            mixed = dot(weights.astype(BF16), v)
            mixed = jnp.where(first, mixed[:BLOCK], mixed[BLOCK:]).astype(BF16)
            at = pl.ds(pl.multiple_of(step * rows + low, BLOCK), BLOCK)
            blended[at, lane : lane + two] = mixed

    @pl.when(step == pl.num_programs(0) - 1)
    def _():
        half = own_ref.shape[0]
        slots = blended.shape[0]
        for out_ref, side in ((own_ref, place[0]), (other_ref, 1 - place[0])):

            @pl.loop(0, half // ROWS)
            def _(i):
                token = lax.broadcasted_iota(jnp.int32, (ROWS, slots), 0) + (side * half + i * ROWS)
                put = jnp.where(token == row_ref[...], 1.0, 0.0).astype(BF16)
                at = pl.ds(pl.multiple_of(i * ROWS, ROWS), ROWS)
                out_ref[at, :] = dot(put, blended[...]).astype(BF16)


def attend(place, frame, video_tokens, order, weight):
    positions, width = video_tokens.shape[1:]
    local = weight.shape[2]
    slots = order.shape[0]
    rows = STEP_BLOCKS * BLOCK
    half = positions // 2
    once = pl.Buffered(1)
    return pl.pallas_call(
        attend_kernel,
        grid_spec=pltpu.PrefetchScalarGridSpec(
            num_scalar_prefetch=1,
            grid=(slots // rows,),
            in_specs=[
                pl.BlockSpec(
                    (1, positions, width), lambda i, s: (frame, 0, 0), pipeline_mode=once
                ),
                pl.BlockSpec((rows, 1), lambda i, s: (i, 0)),
                pl.BlockSpec((1, slots), lambda i, s: (0, 0), pipeline_mode=once),
                pl.BlockSpec((3, width, local), lambda i, s: (0, 0, 0), pipeline_mode=once),
            ],
            out_specs=[pl.BlockSpec((half, local), lambda i, s: (0, 0))] * 2,
            scratch_shapes=[
                pltpu.VMEM((positions, width), BF16),
                pltpu.VMEM((slots, local), BF16),
            ],
        ),
        out_shape=[jax.ShapeDtypeStruct((half, local), BF16)] * 2,
        compiler_params=pltpu.CompilerParams(vmem_limit_bytes=VMEM_LIMIT),
        cost_estimate=pl.CostEstimate(
            flops=2 * slots * width * (positions + 3 * local) + 2 * positions * slots * local,
            bytes_accessed=2 * (positions * (width + local) + 3 * width * local),
            transcendentals=slots * BLOCK * local // HEAD_DIMENSION,
        ),
        name="attend",
    )(place, video_tokens, order[:, None], order[None, :], weight)


def drive_kernel(follows, place, x_ref, own_ref, other_ref, *refs):
    mix_own, mix_a, mix_b, w_own, w_a, w_b, coef, factor = refs[:8]
    before, refs = (refs[8:10], refs[10:]) if follows else (None, refs[8:])
    residual_ref, gate_ref, low_ref, high_ref = refs
    mix = dot(own_ref[...], mix_own[...]).astype(BF16).astype(F32)
    cut = mix_a.shape[0]
    rest = None
    for core, w in ((place[1], mix_a), (1 - place[1], mix_b)):
        term = dot(other_ref[:, pl.ds(pl.multiple_of(core * cut, cut), cut)], w[...])
        rest = term if rest is None else rest + term
    mix = mix + rest.astype(BF16).astype(F32)
    residual = x_ref[0].astype(F32) + mix
    residual_ref[...] = residual
    scale = lax.rsqrt(jnp.mean(residual * residual, axis=-1, keepdims=True) + EPSILON)
    normed = (residual * scale).astype(BF16)
    low, half = 0, low_ref.shape[1]
    for w in (w_own, w_a, w_b):
        high = low + w.shape[2]
        gate_in = jax.nn.sigmoid(dot(normed, w[0]))
        state = coef[:, low:high] * gate_in * dot(normed, w[1])
        out = dot(normed, w[2])
        gate_ref[:, low:high] = (out * jax.nn.sigmoid(out)).astype(BF16)
        side = int(high > half)
        lanes = slice(low - side * half, high - side * half)
        if follows:
            state = state + factor[:, low:high] * before[side][:, lanes].astype(F32)
        (low_ref, high_ref)[side][:, lanes] = state.astype(BF16)
        low = high


def held():
    return pl.BlockSpec(memory_space=pltpu.VMEM)


def drive(place, frame, begin, count, video_tokens, own, other, weights, coef, factor, before):
    positions, width = video_tokens.shape[1:]
    steps = positions // 2 // ROWS
    local = own.shape[1]
    rows, half = count * ROWS, width // 2
    later = pl.BlockSpec((ROWS, half), lambda i, s: (begin + i, 0))
    wide = pl.BlockSpec((ROWS, width), lambda i, s: (i, 0))
    narrow = pl.BlockSpec((ROWS, half), lambda i, s: (i, 0))
    return pl.pallas_call(
        functools.partial(drive_kernel, before is not None),
        grid_spec=pltpu.PrefetchScalarGridSpec(
            num_scalar_prefetch=1,
            grid=(count,),
            in_specs=[
                pl.BlockSpec((1, ROWS, width), lambda i, s: (frame, s[0] * steps + begin + i, 0))
            ]
            + [pl.BlockSpec((ROWS, local), lambda i, s: (begin + i, 0))] * 2
            + [held()] * (len(weights) + 2)
            + [later] * (0 if before is None else 2),
            out_specs=[wide, wide, narrow, narrow],
        ),
        out_shape=[
            jax.ShapeDtypeStruct((rows, width), F32),
            jax.ShapeDtypeStruct((rows, width), BF16),
            jax.ShapeDtypeStruct((rows, half), BF16),
            jax.ShapeDtypeStruct((rows, half), BF16),
        ],
        compiler_params=pltpu.CompilerParams(vmem_limit_bytes=SMALL_LIMIT),
        cost_estimate=pl.CostEstimate(
            flops=8 * rows * width * width,
            bytes_accessed=rows * width * 12,
            transcendentals=2 * rows * width,
        ),
        name="drive",
    )(
        place,
        video_tokens,
        own,
        other,
        *weights,
        coef[frame : frame + 1],
        factor[frame : frame + 1],
        *(() if before is None else before),
    )


def emit_kernel(frames, place, low_ref, high_ref, decay, own, a, b, *refs):
    each, (keep_ref, send_ref) = refs[: 5 * frames], refs[-2:]
    half = low_ref.shape[1]
    incoming = (low_ref[...].astype(F32), high_ref[...].astype(F32))
    parts = [[], []]
    for f in range(frames):
        gate = each[5 * f + 2]
        for side in range(2):
            lanes = slice(side * half, (side + 1) * half)
            state = each[5 * f + side][...].astype(F32)
            state = state + decay[f : f + 1, lanes] * incoming[side]
            parts[side].append((state * gate[:, lanes].astype(F32)).astype(BF16))
    first, second = (jnp.concatenate(p, axis=0) for p in parts)
    cut = a.shape[0]
    for which, out in ((0, keep_ref), (1, send_ref)):
        side = 1 - place[0] if which else place[0]
        lanes = pl.ds(pl.multiple_of(side * half, half), half)
        mix = dot(first, own[:, lanes]).astype(BF16).astype(F32)
        rest = dot(second[:, :cut], a[:, lanes]) + dot(second[:, cut:], b[:, lanes])
        mix = mix + rest.astype(BF16).astype(F32)
        for f in range(frames):
            residual = each[5 * f + 3 + which][...]
            out[f] = (residual + mix[f * ROWS : (f + 1) * ROWS]).astype(BF16)


def emit(place, begin, total, low, high, decay, weights, states, result):
    frames, (rows, half) = len(states), low.shape
    narrow = pl.BlockSpec((ROWS, half), lambda i, s: (i, 0))
    out = pl.BlockSpec((frames, ROWS, half), lambda i, s: (0, i, 0))
    steps = total // 2 // ROWS
    placed = pl.BlockSpec((frames, ROWS, half), lambda i, s: (0, s[0] * steps + begin + i, 0))
    specs, arrays, aliases = [], [], {}
    for f, (residual, gate, low_f, high_f) in enumerate(states):
        at = 0 if f == frames - 1 else begin
        specs += [pl.BlockSpec((ROWS, half), lambda i, s, at=at: (at + i, 0))] * 2
        specs += [
            pl.BlockSpec((ROWS, 2 * half), lambda i, s, at=at: (at + i, 0)),
            pl.BlockSpec((ROWS, half), lambda i, s, at=at: (at + i, s[0])),
            pl.BlockSpec((ROWS, half), lambda i, s, at=at: (at + i, 1 - s[0])),
        ]
        arrays += [low_f, high_f, gate, residual, residual]
    if result is not None:
        aliases = {7 + len(arrays): 0}
        specs.append(pl.BlockSpec(memory_space=pl.ANY))
        arrays.append(result)
    return pl.pallas_call(
        functools.partial(emit_kernel, frames),
        grid_spec=pltpu.PrefetchScalarGridSpec(
            num_scalar_prefetch=1,
            grid=(rows // ROWS,),
            in_specs=[narrow, narrow] + [held()] * 4 + specs,
            out_specs=[placed, out],
        ),
        out_shape=[
            jax.ShapeDtypeStruct((frames, total, half), BF16),
            jax.ShapeDtypeStruct((frames, rows, half), BF16),
        ],
        input_output_aliases=aliases,
        compiler_params=pltpu.CompilerParams(vmem_limit_bytes=SMALL_LIMIT),
        cost_estimate=pl.CostEstimate(
            flops=8 * frames * rows * half * half,
            bytes_accessed=frames * rows * half * 24,
            transcendentals=0,
        ),
        name="emit",
    )(place, low, high, decay, *weights, *arrays)


def swap(value, axis):
    count = lax.axis_size(axis)
    return lax.ppermute(value, axis, [(i, i ^ 1) for i in range(count)])


def shift(value, axis, steps):
    count = lax.axis_size(axis)
    return lax.ppermute(value, axis, [(i, i + steps) for i in range(count - steps)])


def fetch(value, dimension):
    size = value.shape[dimension] // 2
    start = lax.axis_index("clip") * size
    piece = swap(lax.dynamic_slice_in_dim(value, start, size, dimension), "head")
    return piece, swap(piece, "clip")


def incoming_state(low, high, decay, frames):
    odd = lax.axis_index("tm") % 2 == 1
    half = low.shape[1]
    decay_low, decay_high = decay[None, :half], decay[None, half:]
    sent = swap(jnp.where(odd, low, high), "tm")
    decay_sent = swap(jnp.where(odd, decay_low, decay_high), "tm")
    mine = jnp.where(odd, high, low).astype(F32)
    decay_mine = jnp.where(odd, decay_high, decay_low)
    sent = sent.astype(F32)
    earlier, later = jnp.where(odd, sent, mine), jnp.where(odd, mine, sent)
    decay_earlier = jnp.where(odd, decay_sent, decay_mine)
    decay_later = jnp.where(odd, decay_mine, decay_sent)
    both = decay_later * earlier + later
    decay_both = decay_later * decay_earlier
    entering = None if lax.axis_size("tm") > 2 else jnp.zeros_like(both)
    pairs = lax.axis_size("tm") // 2
    for _ in range(min(pairs - 1, -(-(LONGEST_CLIP - 1) // (2 * frames)))):
        total = both if entering is None else both + decay_both * entering
        entering = shift(total.astype(BF16), "tm", 2).astype(F32)
    second = earlier + decay_earlier * entering
    entering, second = entering.astype(BF16), second.astype(BF16)
    got = swap(jnp.where(odd, entering, second), "tm")
    return jnp.where(odd, got, entering), jnp.where(odd, second, got)


def per_device(
    video_tokens,
    window_order,
    clip_id,
    attend_weight,
    attend_out,
    recur_weight,
    frame_decay,
    recur_out,
):
    frames, positions, width = video_tokens.shape
    side = lax.axis_index("head")
    core = lax.axis_index("clip")
    place = jnp.stack([side, core]).astype(jnp.int32)

    out_a, out_b = fetch(attend_out, 0)
    decay_other = swap(frame_decay, "head")
    cut = decay_other.shape[1] // 2
    decay_a, decay_b = decay_other[:, :cut], decay_other[:, cut:]
    frame_decay = jnp.concatenate(
        [
            frame_decay,
            jnp.where(core == 0, decay_a, decay_b),
            jnp.where(core == 0, decay_b, decay_a),
        ],
        axis=1,
    )
    recur_a, recur_b = fetch(recur_weight, 2)

    retain = jnp.exp(frame_decay)
    coef = jnp.sqrt(1.0 - retain * retain)
    previous = shift(clip_id[frames - 1 :], "tm", 1)
    continues = (clip_id == jnp.concatenate([previous, clip_id[:-1]])).astype(F32)
    factor = retain * continues[:, None]
    decay_all = jnp.cumprod(factor, axis=0)

    order = window_order.reshape(frames, positions // PAIR, PAIR)
    order = jnp.pad(order, ((0, 0), (0, 0), (0, BLOCK - PAIR)), constant_values=-1)
    order = order.reshape(frames, -1)
    own, other = [], []
    for f in range(frames):
        placed = order[f]
        if f == 1:
            placed, coef, factor, out_a = lax.optimization_barrier((placed, coef, factor, out_a))
        mine, theirs = attend(place, f, video_tokens, placed, attend_weight)
        if f == 0:
            mine, later_out = lax.optimization_barrier((mine, recur_out))
            emit_a, emit_b = fetch(later_out, 0)
        own.append(mine)
        other.append(swap(theirs, "head"))

    weights = (attend_out, out_a, out_b, recur_weight, recur_a, recur_b)
    coef, emit_a = lax.optimization_barrier((coef, emit_a))
    steps = positions // 2 // ROWS
    cuts = [steps * sum(SHARES[:k]) // sum(SHARES) for k in range(len(SHARES) + 1)]
    states = []
    for f in range(frames - 1):
        before = states[-1][2:] if states else None
        states.append(
            drive(
                place, f, 0, steps, video_tokens, own[f], other[f], weights, coef, factor, before
            )
        )
    before = states[-1][2:] if states else None
    coef, emit_b = lax.optimization_barrier((coef, emit_b))
    result, received = None, []
    for begin, end in zip(cuts, cuts[1:]):
        f = frames - 1
        last = drive(
            place,
            f,
            begin,
            end - begin,
            video_tokens,
            own[f],
            other[f],
            weights,
            coef,
            factor,
            before,
        )
        low, high = incoming_state(last[2], last[3], decay_all[-1], frames)
        result, send = emit(
            place,
            begin,
            positions,
            low,
            high,
            decay_all,
            (recur_out, emit_a, emit_b),
            [*states, last],
            result,
        )
        received.append(swap(send, "head"))
    for begin, part in zip(cuts, received):
        at = (1 - side) * (positions // 2) + begin * ROWS
        result = lax.dynamic_update_slice_in_dim(result, part, at, 1)
    return result


def from_behind(value, axis, steps):
    count = lax.axis_size(axis)
    leading, last = (max(0, -steps), min(count, count - steps))
    return lax.ppermute(value, axis, [(source, source + steps) for source in range(leading, last)])


def prefix_2(value, axis, combine, identity):
    count, position = (lax.axis_size(axis), lax.axis_index(axis))
    everything = jax.tree.map(
        lambda part, kind: lax.all_gather(part.astype(kind), axis),
        value,
        (jnp.bfloat16, jnp.bfloat16),
    )
    start = jax.tree.map(
        lambda part, zero: jnp.broadcast_to(jnp.asarray(zero, part.dtype), part.shape),
        value,
        identity,
    )

    def hop(k, before):
        reached = k < position
        new = combine(
            before, jax.tree.map(lambda part, own: part[k].astype(own.dtype), everything, value)
        )
        return jax.tree.map(lambda a, b: jnp.where(reached, a, b), new, before)

    return lax.fori_loop(0, count, hop, start)


def normalize(values):
    return values * lax.rsqrt(jnp.mean(values * values, axis=-1, keepdims=True) + EPSILON)


def window_attention(queries, keys_all, values_all, window_order):
    frame_count, positions, number_of_heads, head_size = queries.shape
    order_index = window_order[:, :, None, None]

    def arrange(tensor):
        reordered = jnp.take_along_axis(tensor, order_index, axis=1)
        return reordered.reshape(
            frame_count, positions // WINDOW, WINDOW, number_of_heads, head_size
        )

    scores = jnp.einsum(
        "fwihe,fwjhe->fwhij",
        arrange(queries),
        arrange(keys_all),
        preferred_element_type=jnp.float32,
    ) / jnp.sqrt(jnp.float32(head_size))
    weights = jax.nn.softmax(scores, axis=-1).astype(jnp.bfloat16)
    blended = jnp.einsum(
        "fwhij,fwjhe->fwihe", weights, arrange(values_all), preferred_element_type=jnp.float32
    ).astype(jnp.bfloat16)
    blended = blended.reshape(frame_count, positions, number_of_heads, head_size)
    inverse = jnp.argsort(window_order, axis=1)
    return jnp.take_along_axis(blended, inverse[:, :, None, None], axis=1)


def per_device_any(
    video_tokens,
    window_order,
    clip_id,
    attend_weight,
    attend_out,
    recur_weight,
    frame_decay,
    recur_out,
):
    frame_count, positions, model_width = video_tokens.shape
    local_width = attend_weight.shape[2]
    row_count = frame_count * positions
    inputs = video_tokens.reshape(row_count, model_width).astype(jnp.float32)
    normed = normalize(inputs).astype(jnp.bfloat16)
    projected = jnp.einsum(
        "td,kde->kte", normed, attend_weight, preferred_element_type=jnp.float32
    ).astype(jnp.bfloat16)
    shaped = projected.reshape(
        3, frame_count, positions, local_width // HEAD_DIMENSION, HEAD_DIMENSION
    )
    attended = window_attention(shaped[0], shaped[1], shaped[2], window_order).reshape(
        row_count, local_width
    )
    partial_mix = jnp.dot(attended, attend_out, preferred_element_type=jnp.float32)
    offset = lax.axis_index("head") * local_width
    residual = inputs + lax.psum(partial_mix.astype(jnp.bfloat16), "head").astype(jnp.float32)
    normed_again = normalize(residual).astype(jnp.bfloat16)
    recur_proj = jnp.einsum(
        "td,kde->kte", normed_again, recur_weight, preferred_element_type=jnp.float32
    )
    residual_own = lax.dynamic_slice_in_dim(residual, offset, local_width, 1)
    gate_in = jax.nn.sigmoid(recur_proj[0]).reshape(frame_count, positions, local_width)
    value_in = recur_proj[1].reshape(frame_count, positions, local_width)
    out_gate = jax.nn.silu(recur_proj[2]).reshape(frame_count, positions, local_width)
    retain = jnp.exp(frame_decay)
    driven = jnp.sqrt(1.0 - retain * retain)[:, None, :] * gate_in * value_in
    previous = from_behind(clip_id[frame_count - 1 :], "tm", 1)
    continues = jnp.concatenate(
        [
            (clip_id[:1] == previous).astype(jnp.float32),
            (clip_id[1:] == clip_id[:-1]).astype(jnp.float32),
        ]
    )
    factor = retain * continues[:, None]

    def advance(carried, inputs_now):
        decay_total, state_now = carried
        factor_now, driven_now = inputs_now
        decay_total = factor_now * decay_total
        state_now = factor_now[None, :] * state_now + driven_now
        return ((decay_total, state_now), (decay_total, state_now))

    start_carry = (
        jnp.ones((local_width,), jnp.float32),
        jnp.zeros((positions, local_width), jnp.float32),
    )
    last_carry, all_carry = lax.scan(advance, start_carry, (factor, driven))
    decay_last, state_last = last_carry
    decay_all, state_all = all_carry

    def combine(earlier, later_part):
        return (later_part[0] * earlier[0], later_part[0][None, :] * earlier[1] + later_part[1])

    prefix = prefix_2(
        (decay_last, state_last),
        "tm",
        combine,
        (jnp.ones_like(decay_last), jnp.zeros_like(state_last)),
    )
    incoming = prefix[1]
    states = state_all + decay_all[:, None, :] * incoming[None, :, :]
    output_rows = (states * out_gate).astype(jnp.bfloat16).reshape(row_count, local_width)
    partial_out = jnp.dot(output_rows, recur_out, preferred_element_type=jnp.float32)
    result = residual_own + lax.psum_scatter(
        partial_out.astype(jnp.bfloat16), "head", scatter_dimension=1, tiled=True
    ).astype(jnp.float32)
    return result.astype(jnp.bfloat16).reshape(frame_count, positions, local_width)


def solution(mesh):
    halves = mesh.shape["head"] == 2 and mesh.shape["clip"] == 2 and mesh.shape["tm"] % 2 == 0
    return jax.shard_map(
        per_device if halves else per_device_any,
        mesh=mesh,
        in_specs=(
            P(("clip", "tm"), None, None),
            P(("clip", "tm"), None),
            P(("clip", "tm")),
            P(None, None, "head"),
            P("head", None),
            P(None, None, "head"),
            P(("clip", "tm"), "head"),
            P("head", None),
        ),
        out_specs=P(("clip", "tm"), None, "head"),
        check_vma=False,
    )
```
